32 devices in a mesh: rows: 16 (over z, x, core), split: 2 (over y).
Axes of the slice: x: 2, y: 2, z: 4, core: 2. Of those that a mesh axis runs over, the one named last changes fastest.
Arguments:
- embeddings: bfloat16 [8192, 768], P(('rows', 'split')), may hold values from -24 to 24
- cluster_id: int32 [8192], P(('rows', 'split')), may hold values from 0 to 127, as said below
- owner_map: int32 [128], replicated, may hold values from 0 to 15, as said below
Outputs:
- prune_score: float32 [8192], P(('rows', 'split'))
The draws below stay inside these ranges and needn't reach their ends.
Inputs may be any that keep to these rules, and one draw needn't show every extreme that they name: `owner_map`: every group 0 to 15 holds exactly 8 clusters. `cluster_id`: within each aligned block of 256 rows (the rows of one device), no group holds more than 32 of the block's rows, and one group holds exactly 32; every group holds exactly 32 rows of some block. Every cluster holds two rows or more.
All inputs are finite; a program needn't handle non-finite values.
Results may differ from the reference program's by a relative error of at most 0.0005.
Values may be sent and summed in bfloat16 or wider, within the bound.
A program may use at most 64 MiB of HBM per device.

```python
import math
import jax
import jax.numpy as jnp
from jax import lax

D = 768
ROW_DEV = 256
CL_DEV = 8
CAP = 32
CLUSTERS = 128
ROWS = 8192


def group_permutation(key):
    return jax.random.permutation(jax.random.fold_in(key, 11), CLUSTERS)


def cluster_layout(key):
    owners = CLUSTERS // CL_DEV
    blocks = ROWS // ROW_DEV
    inverse = jnp.argsort(group_permutation(key))
    offset = jax.random.randint(jax.random.fold_in(key, 12), (), 0, owners)
    block_range = jnp.arange(blocks)
    full_owner = (block_range + offset) % owners
    pair_shift = block_range // owners * (CAP // 2)
    block_keys = jax.random.split(jax.random.fold_in(key, 13), blocks)

    def one_block(block_key, chosen, shift):
        first_key, second_key, third_key = jax.random.split(block_key, 3)
        others = jax.random.permutation(first_key, (owners - 1) * CAP)[:ROW_DEV - CAP] // CAP
        others = others + (others >= chosen).astype(others.dtype)
        listed = jnp.concatenate([jnp.full((CAP,), chosen, others.dtype), others])
        paired = ((jnp.arange(CAP) // 2 + shift) % CL_DEV).astype(jnp.int32)
        loose = jax.random.randint(third_key, (ROW_DEV - CAP,), 0, CL_DEV).astype(jnp.int32)
        member = jnp.concatenate([paired, loose])
        order = jax.random.permutation(second_key, ROW_DEV)
        return inverse[listed[order] * CL_DEV + member[order]]
    return jax.vmap(one_block)(block_keys, full_owner, pair_shift).reshape(-1).astype(jnp.int32)


def draw_owner_map(key, part):
    return (group_permutation(key) // CL_DEV).astype(jnp.int32)


def draw_cluster_id(key, part):
    return cluster_layout(key)


def draw_embeddings(key, part):
    clusters = cluster_layout(key)
    centre_key = jax.random.fold_in(key, 21)
    spread_key = jax.random.fold_in(key, 22)
    noise_key = jax.random.fold_in(key, 23)
    centres = 0.35 * jnp.clip(jax.random.normal(centre_key, (CLUSTERS, D), jnp.float32), -6.0, 6.0)
    spread = jnp.exp(jax.random.uniform(spread_key, (ROWS, 1), jnp.float32, math.log(0.5), math.log(2.0)))
    noise_rows = jnp.clip(jax.random.normal(noise_key, (ROWS, D), jnp.float32), -6.0, 6.0)
    return (centres[clusters] + spread * noise_rows).astype(jnp.bfloat16)


def setup_inputs(seed: int = 0) -> dict:
    seeds = jax.random.split(jax.random.key(seed), 4)
    return {
        "embeddings": draw_embeddings(jax.random.fold_in(seeds[3], 71), 0),
        "cluster_id": draw_cluster_id(jax.random.fold_in(seeds[3], 71), 0),
        "owner_map": draw_owner_map(jax.random.fold_in(seeds[3], 71), 0),
    }


FLOOR_SCORE = -1e+30

def reference(embeddings, cluster_id, owner_map):
    owners = CLUSTERS // CL_DEV
    blocks = ROWS // ROW_DEV
    owner_of = owner_map[cluster_id]
    by_block = owner_of.reshape(blocks, ROW_DEV)
    earlier = jnp.arange(ROW_DEV)[None, :] < jnp.arange(ROW_DEV)[:, None]
    ranking = lax.optimization_barrier(jnp.sum((by_block[:, :, None] == by_block[:, None, :]) & earlier[None], axis=2))
    placing = (jnp.arange(blocks, dtype=jnp.int32)[:, None] * CAP + ranking.astype(jnp.int32)).reshape(-1)
    member_table = jnp.full((owners, blocks * CAP), -1, jnp.int32).at[owner_of, placing].set(jnp.arange(ROWS, dtype=jnp.int32))
    score_scale = 1.0 / math.sqrt(D)

    def one_group(members):
        present = members >= 0
        clipped = jnp.maximum(members, 0)
        member_rows = embeddings[clipped]
        member_ids = jnp.where(present, cluster_id[clipped], -1)
        scores = jnp.dot(member_rows, member_rows.T, preferred_element_type=jnp.float32) * score_scale
        group_size = members.shape[0]
        same_cluster = member_ids[:, None] == member_ids[None, :]
        allowed = present[None, :] & same_cluster & (jnp.arange(group_size)[:, None] != jnp.arange(group_size)[None, :])
        masked = jnp.where(allowed, scores, FLOOR_SCORE)
        highest = lax.optimization_barrier(jnp.max(masked, axis=1))
        totals = lax.optimization_barrier(jnp.sum(jnp.where(allowed, jnp.exp(masked - highest[:, None]), 0.0), axis=1))
        return highest + jnp.log(totals)
    density = lax.map(one_group, member_table)
    flat_members = member_table.reshape(-1)
    flat_density = density.reshape(-1)
    present = flat_members >= 0
    member_cluster = jnp.where(present, cluster_id[jnp.maximum(flat_members, 0)], CLUSTERS)
    sum_density = jax.ops.segment_sum(jnp.where(present, flat_density, 0.0), member_cluster, CLUSTERS + 1)[:CLUSTERS]
    counts = jax.ops.segment_sum(present.astype(jnp.float32), member_cluster, CLUSTERS + 1)[:CLUSTERS]
    cluster_mean = sum_density / jnp.maximum(counts, 1.0)
    scores_out = jnp.where(present, flat_density - cluster_mean[jnp.minimum(member_cluster, CLUSTERS - 1)], 0.0)
    target = jnp.where(present, flat_members, ROWS)
    return jnp.zeros((ROWS + 1,), jnp.float32).at[target].set(scores_out)[:ROWS]
```

```python
import functools

import jax
import jax.numpy as jnp
from jax import lax
from jax.experimental import pallas as pl
from jax.experimental.pallas import tpu as pltpu
from jax.sharding import PartitionSpec as P

FLOOR_SCORE = -1e30
LANES = 128
KEY_CHUNK = 256
MESH = pl.DeviceIdType.MESH
F32 = jnp.float32
BF16 = jnp.bfloat16


def iota(shape, dim):
    return lax.broadcasted_iota(jnp.int32, shape, dim)


def one_hot(hit, dtype=BF16):
    return jnp.where(hit, 1.0, 0.0).astype(dtype)


def dot(a, b, dims=((1,), (0,)), precision=None):
    return lax.dot_general(a, b, (dims, ((), ())), preferred_element_type=F32, precision=precision)


def column_to_row(column):
    blocks = [
        jnp.transpose(jnp.broadcast_to(column[at : at + LANES], (LANES, LANES)))[0:1]
        for at in range(0, column.shape[0], LANES)
    ]
    return jnp.concatenate(blocks, axis=1)


def kernel(
    groups, parts, local_clusters,
    emb_ref, cid_ref, owner_ref, out_ref,
    outgoing, out_ids, keys, key_ids, id_rows, id_cols, scores, sums, result, returned,
    send_sem, recv_sem, id_send, id_recv, fwd_send, fwd_recv, idf_send, idf_recv,
    sum_send, sum_recv, ret_send, ret_recv, local_sem,
):
    rows_here, width = emb_ref.shape
    clusters_all = owner_ref.shape[1]
    cap = outgoing.shape[1]
    per_row = LANES // cap
    slots = groups * cap
    lane_rows = slots // LANES
    r, s = lax.axis_index("rows"), lax.axis_index("split")
    me = (r // parts) * parts + s
    part = r % parts

    def device(group, piece):
        return ((group // parts) * parts + piece, group % parts)

    def step_offset(t):
        half = (t + 1) // 2
        return groups // 2 + half - 2 * half * ((t + 1) % 2)

    def peer_out(t):
        return (me + step_offset(t)) % groups

    def peer_in(t):
        return (me + groups - step_offset(t)) % groups

    def sibling(d):
        return (part + d) % parts

    barrier = pltpu.get_barrier_semaphore()

    @pl.loop(0, groups - 1)
    def _(t):
        pl.semaphore_signal(barrier, inc=1, device_id=device(peer_out(t), part), device_id_type=MESH)

    for d in range(1, parts):
        pl.semaphore_signal(barrier, inc=1, device_id=device(me, sibling(d)), device_id_type=MESH)

    cid = cid_ref[...]
    cluster_hit = one_hot(iota((clusters_all, rows_here), 0) == cid)
    owner_cl = iota((groups, clusters_all), 0) == owner_ref[...]
    owner_cl_hot = one_hot(owner_cl)
    before_cl = one_hot(iota((clusters_all, clusters_all), 0) < iota((clusters_all, clusters_all), 1))
    local_rank = dot(owner_cl_hot, before_cl)
    label_cl = jnp.where(owner_cl, local_rank + 1.0, 0.0).astype(BF16)
    labels = dot(label_cl, cluster_hit)
    owner_hot = jnp.where(labels > 0.5, 1.0, 0.0)
    before = one_hot(iota((rows_here, rows_here), 0) < iota((rows_here, rows_here), 1))
    prefix = dot(owner_hot.astype(BF16), before)
    rank = jnp.sum(owner_hot * prefix, axis=0, keepdims=True).astype(jnp.int32)
    lane_hit = one_hot(iota((LANES, rows_here), 0) == rank + (me % per_row) * cap, F32)
    id_block = dot(labels.astype(BF16), lane_hit.astype(BF16), ((1,), (1,)))
    for g in range(groups):
        out_ids[g] = id_block[g : g + 1]
    rank_hot = one_hot(iota((cap, rows_here), 0) == rank, F32)
    emb = emb_ref[...]
    per_step = max(1, 256 // cap)
    for g0 in range(0, groups, per_step):
        placed = jnp.concatenate(
            [(rank_hot * owner_hot[g : g + 1]).astype(BF16) for g in range(g0, min(g0 + per_step, groups))], axis=0
        )
        outgoing[g0 : g0 + per_step] = dot(placed, emb).astype(BF16).reshape(per_step, cap, width)

    def row_copy(to, frm):
        return pltpu.make_async_remote_copy(
            src_ref=outgoing.at[to], dst_ref=keys.at[part, me],
            send_sem=send_sem.at[to], recv_sem=recv_sem.at[frm],
            device_id=device(to, part), device_id_type=MESH,
        )

    def id_copy(to, frm):
        return pltpu.make_async_remote_copy(
            src_ref=out_ids.at[to], dst_ref=key_ids.at[part, me],
            send_sem=id_send.at[to], recv_sem=id_recv.at[frm],
            device_id=device(to, part), device_id_type=MESH,
        )

    def forward(q, piece, d, home):
        return pltpu.make_async_remote_copy(
            src_ref=keys.at[home, q], dst_ref=keys.at[home, q],
            send_sem=fwd_send.at[d, q], recv_sem=fwd_recv.at[home, q],
            device_id=device(me, piece), device_id_type=MESH,
        )

    def forward_ids(piece, d, home):
        return pltpu.make_async_remote_copy(
            src_ref=key_ids.at[home], dst_ref=key_ids.at[home],
            send_sem=idf_send.at[d], recv_sem=idf_recv.at[home],
            device_id=device(me, piece), device_id_type=MESH,
        )

    pl.semaphore_wait(barrier, groups + parts - 2)

    @pl.loop(0, groups - 1)
    def _(t):
        to = peer_out(t)
        id_copy(to, me).start()
        row_copy(to, me).start()

    own_rows = pltpu.make_async_copy(outgoing.at[me], keys.at[part, me], local_sem.at[0])
    own_ids = pltpu.make_async_copy(out_ids.at[me], key_ids.at[part, me], local_sem.at[1])
    own_rows.start()
    own_ids.start()
    own_rows.wait()
    own_ids.wait()
    for d in range(1, parts):
        forward(me, sibling(d), d, part).start()

    @pl.loop(0, groups - 1)
    def _(t):
        q = peer_in(t)
        row_copy(q, q).wait_recv()
        for d in range(1, parts):
            forward(q, sibling(d), d, part).start()

    @pl.loop(0, groups - 1)
    def _(t):
        q = peer_in(t)
        id_copy(q, q).wait_recv()

    for d in range(1, parts):
        forward_ids(sibling(d), d, part).start()
    for d in range(1, parts):
        home = sibling(d)
        forward_ids(home, d, home).wait_recv()

    for piece in range(parts):
        for l in range(lane_rows):
            row = key_ids[piece, l * per_row]
            for j in range(1, per_row):
                row = row + key_ids[piece, l * per_row + j]
            id_rows[piece, l] = row
    query_rows = []
    for l in range(lane_rows):
        row = id_rows[part, l]
        query_rows.append(row)
        id_cols[l * LANES : (l + 1) * LANES] = jnp.transpose(jnp.broadcast_to(row, (LANES, LANES)))

    for d in range(1, parts):
        home = sibling(d)

        @pl.loop(0, groups)
        def _(q):
            forward(q, home, d, home).wait_recv()

    scale = 1.0 / width**0.5
    chunk_groups = KEY_CHUNK // cap
    chunk_lanes = KEY_CHUNK // LANES
    per_piece = groups // chunk_groups
    n_chunks = parts * per_piece

    queries = keys[part].reshape(slots, width)
    id_col = jnp.concatenate([id_cols[...]] * chunk_lanes, axis=1)
    gap = iota((slots, KEY_CHUNK), 0) - iota((slots, KEY_CHUNK), 1)

    def score_chunk(j, high):
        piece, at = j // per_piece, j % per_piece
        block = keys[piece, pl.ds(at * chunk_groups, chunk_groups)].reshape(KEY_CHUNK, width)
        raw = dot(queries, block, ((1,), (1,))) * scale
        id_row = jnp.concatenate([id_rows[piece, at * chunk_lanes + i] for i in range(chunk_lanes)], axis=1)
        own_gap = (piece - part) * slots + at * KEY_CHUNK
        masked = jnp.where((id_col == id_row) & (gap != own_gap), raw, FLOOR_SCORE)
        scores[j] = masked
        folded = masked[:, :LANES]
        for i in range(1, chunk_lanes):
            folded = jnp.maximum(folded, masked[:, i * LANES : (i + 1) * LANES])
        return jnp.maximum(high, folded)

    high = lax.fori_loop(
        0, n_chunks, score_chunk, jnp.full((slots, LANES), FLOOR_SCORE, F32), unroll=n_chunks <= 4
    )
    highest = jnp.max(high, axis=1, keepdims=True)

    def sum_chunk(j, total):
        value = jnp.exp(scores[j] - highest)
        for i in range(chunk_lanes):
            total = total + value[:, i * LANES : (i + 1) * LANES]
        return total

    total = lax.fori_loop(0, n_chunks, sum_chunk, jnp.zeros((slots, LANES), F32), unroll=n_chunks <= 4)
    density = column_to_row(highest + jnp.log(jnp.sum(total, axis=1, keepdims=True)))
    labels_row = jnp.concatenate(query_rows, axis=1)
    member = labels_row == (iota((local_clusters, slots), 0) + 1).astype(F32)
    part_sum = jnp.sum(jnp.where(member, density, 0.0), axis=1, keepdims=True)
    part_count = jnp.sum(jnp.where(member, 1.0, 0.0), axis=1, keepdims=True)
    sums[part] = jnp.where(iota((local_clusters, LANES), 1) == 0, part_sum, part_count)

    def sum_copy(piece, d, home):
        return pltpu.make_async_remote_copy(
            src_ref=sums.at[home], dst_ref=sums.at[home],
            send_sem=sum_send.at[d], recv_sem=sum_recv.at[home],
            device_id=device(me, piece), device_id_type=MESH,
        )

    for d in range(1, parts):
        sum_copy(sibling(d), d, part).start()
    for d in range(1, parts):
        home = sibling(d)
        sum_copy(home, d, home).wait_recv()
    both = sums[0]
    for piece in range(1, parts):
        both = both + sums[piece]
    mean = both[:, 0:1] / jnp.maximum(both[:, 1:2], 1.0)
    row_mean = jnp.sum(jnp.where(member, mean, 0.0), axis=0, keepdims=True)
    final = jnp.where(labels_row > 0.5, density - row_mean, 0.0)
    for l in range(lane_rows):
        result[l] = final[:, l * LANES : (l + 1) * LANES]

    def ret_copy(to, frm):
        return pltpu.make_async_remote_copy(
            src_ref=result.at[to // per_row], dst_ref=returned.at[me],
            send_sem=ret_send.at[to], recv_sem=ret_recv.at[frm],
            device_id=device(to, part), device_id_type=MESH,
        )

    @pl.loop(0, groups - 1)
    def _(t):
        ret_copy(peer_out(t), me).start()

    own_ret = pltpu.make_async_copy(result.at[me // per_row], returned.at[me], local_sem.at[2])
    own_ret.start()
    own_ret.wait()

    @pl.loop(0, groups - 1)
    def _(t):
        q = peer_in(t)
        id_copy(q, q).wait_send()
        row_copy(q, q).wait_send()

    for d in range(1, parts):
        forward_ids(sibling(d), d, part).wait_send()
        sum_copy(sibling(d), d, part).wait_send()

        @pl.loop(0, groups)
        def _(q):
            forward(q, sibling(d), d, part).wait_send()

    @pl.loop(0, groups - 1)
    def _(t):
        q = peer_in(t)
        ret_copy(q, q).wait_recv()

    back = jnp.concatenate([returned[g] for g in range(groups)], axis=0)
    picked = dot(back, lane_hit, precision=lax.Precision.HIGHEST)
    out_ref[...] = jnp.sum(owner_hot * picked, axis=0, keepdims=True)

    @pl.loop(0, groups - 1)
    def _(t):
        q = peer_in(t)
        ret_copy(q, q).wait_send()


def on_device(embeddings, cluster_id, owner_map):
    rows_here, width = embeddings.shape
    clusters_all = owner_map.shape[0]
    groups = lax.axis_size("rows")
    parts = lax.axis_size("split")
    cap = 2 * rows_here // groups
    slots = groups * cap
    lane_rows = slots // LANES
    local_clusters = clusters_all // groups
    dma = pltpu.SemaphoreType.DMA
    vmem = pl.BlockSpec(memory_space=pltpu.VMEM)
    out = pl.pallas_call(
        functools.partial(kernel, groups, parts, local_clusters),
        out_shape=jax.ShapeDtypeStruct((1, rows_here), F32),
        in_specs=[vmem] * 3,
        out_specs=vmem,
        scratch_shapes=[
            pltpu.VMEM((groups, cap, width), BF16),
            pltpu.VMEM((groups, 1, LANES), F32),
            pltpu.VMEM((parts, groups, cap, width), BF16),
            pltpu.VMEM((parts, groups, 1, LANES), F32),
            pltpu.VMEM((parts, lane_rows, 1, LANES), F32),
            pltpu.VMEM((slots, LANES), F32),
            pltpu.VMEM((parts * slots // KEY_CHUNK, slots, KEY_CHUNK), F32),
            pltpu.VMEM((parts, local_clusters, LANES), F32),
            pltpu.VMEM((lane_rows, 1, LANES), F32),
            pltpu.VMEM((groups, 1, LANES), F32),
            dma((groups,)), dma((groups,)), dma((groups,)), dma((groups,)),
            dma((parts, groups)), dma((parts, groups)), dma((parts,)), dma((parts,)),
            dma((parts,)), dma((parts,)), dma((groups,)), dma((groups,)), dma((3,)),
        ],
        compiler_params=pltpu.CompilerParams(
            collective_id=0, has_side_effects=True, vmem_limit_bytes=60 * 1024 * 1024
        ),
        name="soft_neighbour",
    )(embeddings, cluster_id.reshape(1, rows_here), owner_map.reshape(1, clusters_all))
    return out.reshape(rows_here)


def solution(mesh):
    placed = (P(("rows", "split"), None), P(("rows", "split")), P())
    return jax.shard_map(
        on_device, mesh=mesh, in_specs=placed, out_specs=P(("rows", "split")), check_vma=False
    )
```

```python
import functools

import jax
import jax.numpy as jnp
from jax import lax
from jax.experimental import pallas as pl
from jax.experimental.pallas import tpu as pltpu
from jax.sharding import PartitionSpec as P

FLOOR_SCORE = -1e30
LANES = 128
KEY_CHUNK = 256
PLANE = 4
MESH = pl.DeviceIdType.MESH
F32 = jnp.float32
BF16 = jnp.bfloat16


def iota(shape, dim):
    return lax.broadcasted_iota(jnp.int32, shape, dim)


def one_hot(hit, dtype=BF16):
    return jnp.where(hit, 1.0, 0.0).astype(dtype)


def dot(a, b, dims=((1,), (0,)), precision=None):
    return lax.dot_general(a, b, (dims, ((), ())), preferred_element_type=F32, precision=precision)


def column_to_row(column):
    blocks = [
        jnp.transpose(jnp.broadcast_to(column[at : at + LANES], (LANES, LANES)))[0:1]
        for at in range(0, column.shape[0], LANES)
    ]
    return jnp.concatenate(blocks, axis=1)


def kernel(
    groups, parts, local_clusters,
    emb_ref, cid_ref, owner_ref, out_ref,
    outgoing, out_ids, keys, key_ids, id_rows, id_cols, scores, sums, result, returned,
    send_sem, recv_sem, id_send, id_recv, fwd_send, fwd_recv, idf_send, idf_recv,
    sum_send, sum_recv, ret_send, ret_recv, local_sem, diag_sem, up_sem, down_sem,
):
    rows_here, width = emb_ref.shape
    clusters_all = owner_ref.shape[1]
    cap = outgoing.shape[1]
    per_row = LANES // cap
    slots = groups * cap
    lane_rows = slots // LANES
    r, s = lax.axis_index("rows"), lax.axis_index("split")
    me = (r // parts) * parts + s
    part = r % parts

    def device(group, piece):
        return ((group // parts) * parts + piece, group % parts)

    def step_offset(t):
        half = (t + 1) // 2
        return groups // 2 + half - 2 * half * ((t + 1) % 2)

    def peer_out(t):
        return (me + step_offset(t)) % groups

    def peer_in(t):
        return (me + groups - step_offset(t)) % groups

    def sibling(d):
        return (part + d) % parts

    barrier = pltpu.get_barrier_semaphore()

    levels = groups // PLANE
    z, a, b = me // PLANE, me // 2 % 2, me % 2

    def group_at(level, da, db):
        return level * PLANE + (a + da) % 2 * 2 + (b + db) % 2

    def tell(semaphore, group):
        pl.semaphore_signal(semaphore, inc=1, device_id=device(group, part), device_id_type=MESH)

    def beside(level, action):
        @pl.when((level >= 0) & (level < levels))
        def _():
            action()

    tell(barrier, group_at(z, 1, 0))
    tell(barrier, group_at(z, 0, 1))
    beside(z - 1, lambda: tell(barrier, group_at(z - 1, 0, 0)))
    beside(z + 1, lambda: tell(barrier, group_at(z + 1, 0, 0)))
    for d in range(1, parts):
        pl.semaphore_signal(barrier, inc=1, device_id=device(me, sibling(d)), device_id_type=MESH)

    cid = cid_ref[...]
    cluster_hit = one_hot(iota((clusters_all, rows_here), 0) == cid)
    owner_cl = iota((groups, clusters_all), 0) == owner_ref[...]
    owner_cl_hot = one_hot(owner_cl)
    before_cl = one_hot(iota((clusters_all, clusters_all), 0) < iota((clusters_all, clusters_all), 1))
    local_rank = dot(owner_cl_hot, before_cl)
    label_cl = jnp.where(owner_cl, local_rank + 1.0, 0.0).astype(BF16)
    labels = dot(label_cl, cluster_hit)
    owner_hot = jnp.where(labels > 0.5, 1.0, 0.0)
    before = one_hot(iota((rows_here, rows_here), 0) < iota((rows_here, rows_here), 1))
    prefix = dot(owner_hot.astype(BF16), before)
    rank = jnp.sum(owner_hot * prefix, axis=0, keepdims=True).astype(jnp.int32)
    lane_hit = one_hot(iota((LANES, rows_here), 0) == rank + (me % per_row) * cap, F32)
    id_block = dot(labels.astype(BF16), lane_hit.astype(BF16), ((1,), (1,)))
    for g in range(groups):
        out_ids[g] = id_block[g : g + 1]
    rank_hot = one_hot(iota((cap, rows_here), 0) == rank, F32)
    emb = emb_ref[...]
    per_step = max(1, 256 // cap)
    for g0 in range(0, groups, per_step):
        placed = jnp.concatenate(
            [(rank_hot * owner_hot[g : g + 1]).astype(BF16) for g in range(g0, min(g0 + per_step, groups))], axis=0
        )
        outgoing[g0 : g0 + per_step] = dot(placed, emb).astype(BF16).reshape(per_step, cap, width)

    def row_copy(to, frm):
        return pltpu.make_async_remote_copy(
            src_ref=outgoing.at[to], dst_ref=keys.at[part, me],
            send_sem=send_sem.at[to], recv_sem=recv_sem.at[frm],
            device_id=device(to, part), device_id_type=MESH,
        )

    def id_copy(to, frm):
        return pltpu.make_async_remote_copy(
            src_ref=out_ids.at[to], dst_ref=key_ids.at[part, me],
            send_sem=id_send.at[to], recv_sem=id_recv.at[frm],
            device_id=device(to, part), device_id_type=MESH,
        )

    def forward(q, piece, d, home):
        return pltpu.make_async_remote_copy(
            src_ref=keys.at[home, q], dst_ref=keys.at[home, q],
            send_sem=fwd_send.at[d, q], recv_sem=fwd_recv.at[home, q],
            device_id=device(me, piece), device_id_type=MESH,
        )

    def forward_ids(piece, d, home):
        return pltpu.make_async_remote_copy(
            src_ref=key_ids.at[home], dst_ref=key_ids.at[home],
            send_sem=idf_send.at[d], recv_sem=idf_recv.at[home],
            device_id=device(me, piece), device_id_type=MESH,
        )

    def send(group):
        id_copy(group, me).start()
        row_copy(group, me).start()

    pl.semaphore_wait(
        barrier, parts + 1 + jnp.where(z > 0, 1, 0) + jnp.where(z < levels - 1, 1, 0)
    )
    beside(z - 1, lambda: send(group_at(z - 1, 0, 0)))
    beside(z + 1, lambda: send(group_at(z + 1, 0, 0)))
    tell(diag_sem, group_at(z, 1, 0))
    send(group_at(z, 1, 0))
    send(group_at(z, 0, 1))
    pl.semaphore_wait(diag_sem, 1)
    beside(z + 1, lambda: tell(up_sem.at[1], group_at(z + 1, 0, 0)))
    beside(z - 1, lambda: tell(down_sem.at[1], group_at(z - 1, 0, 0)))
    send(group_at(z, 1, 1))

    @pl.loop(1, levels, unroll=levels <= 4)
    def _(d):
        def reach(ready, level, onward):
            pl.semaphore_wait(ready.at[d], 1)
            beside(onward, lambda: tell(ready.at[d + 1], group_at(onward, 0, 0)))

            @pl.when(d > 1)
            def _():
                send(group_at(level, 0, 0))

            for da, db in ((1, 0), (0, 1), (1, 1)):
                send(group_at(level, da, db))

        beside(z - d, lambda: reach(up_sem, z - d, z + 1))
        beside(z + d, lambda: reach(down_sem, z + d, z - 1))

    own_rows = pltpu.make_async_copy(outgoing.at[me], keys.at[part, me], local_sem.at[0])
    own_ids = pltpu.make_async_copy(out_ids.at[me], key_ids.at[part, me], local_sem.at[1])
    own_rows.start()
    own_ids.start()
    own_rows.wait()
    own_ids.wait()
    for d in range(1, parts):
        forward(me, sibling(d), d, part).start()

    def take(q):
        row_copy(q, q).wait_recv()
        for d in range(1, parts):
            forward(q, sibling(d), d, part).start()

    for da, db in ((1, 0), (0, 1), (1, 1)):
        take(group_at(z, da, db))

    @pl.loop(1, levels, unroll=levels <= 4)
    def _(d):
        def take_level(level):
            for da, db in ((0, 0), (1, 0), (0, 1), (1, 1)):
                take(group_at(level, da, db))

        beside(z - d, lambda: take_level(z - d))
        beside(z + d, lambda: take_level(z + d))

    @pl.loop(0, groups - 1, unroll=groups <= 16)
    def _(t):
        q = peer_in(t)
        id_copy(q, q).wait_recv()

    for d in range(1, parts):
        forward_ids(sibling(d), d, part).start()
    for d in range(1, parts):
        home = sibling(d)
        forward_ids(home, d, home).wait_recv()

    for piece in range(parts):
        for l in range(lane_rows):
            row = key_ids[piece, l * per_row]
            for j in range(1, per_row):
                row = row + key_ids[piece, l * per_row + j]
            id_rows[piece, l] = row
    query_rows = []
    for l in range(lane_rows):
        row = id_rows[part, l]
        query_rows.append(row)
        id_cols[l * LANES : (l + 1) * LANES] = jnp.transpose(jnp.broadcast_to(row, (LANES, LANES)))

    for d in range(1, parts):
        home = sibling(d)

        @pl.loop(0, groups, unroll=groups <= 16)
        def _(q):
            forward(q, home, d, home).wait_recv()

    scale = 1.0 / width**0.5
    chunk_groups = KEY_CHUNK // cap
    chunk_lanes = KEY_CHUNK // LANES
    per_piece = groups // chunk_groups
    n_chunks = parts * per_piece

    queries = keys[part].reshape(slots, width)
    id_col = jnp.concatenate([id_cols[...]] * chunk_lanes, axis=1)
    gap = iota((slots, KEY_CHUNK), 0) - iota((slots, KEY_CHUNK), 1)

    def score_chunk(j, high):
        piece, at = j // per_piece, j % per_piece
        block = keys[piece, pl.ds(at * chunk_groups, chunk_groups)].reshape(KEY_CHUNK, width)
        raw = dot(queries, block, ((1,), (1,))) * scale
        id_row = jnp.concatenate([id_rows[piece, at * chunk_lanes + i] for i in range(chunk_lanes)], axis=1)
        own_gap = (piece - part) * slots + at * KEY_CHUNK
        masked = jnp.where((id_col == id_row) & (gap != own_gap), raw, FLOOR_SCORE)
        scores[j] = masked
        folded = masked[:, :LANES]
        for i in range(1, chunk_lanes):
            folded = jnp.maximum(folded, masked[:, i * LANES : (i + 1) * LANES])
        return jnp.maximum(high, folded)

    high = lax.fori_loop(
        0, n_chunks, score_chunk, jnp.full((slots, LANES), FLOOR_SCORE, F32), unroll=n_chunks <= 4
    )
    highest = jnp.max(high, axis=1, keepdims=True)

    def sum_chunk(j, total):
        value = jnp.exp(scores[j] - highest)
        for i in range(chunk_lanes):
            total = total + value[:, i * LANES : (i + 1) * LANES]
        return total

    total = lax.fori_loop(0, n_chunks, sum_chunk, jnp.zeros((slots, LANES), F32), unroll=n_chunks <= 4)
    density = column_to_row(highest + jnp.log(jnp.sum(total, axis=1, keepdims=True)))
    labels_row = jnp.concatenate(query_rows, axis=1)
    member = labels_row == (iota((local_clusters, slots), 0) + 1).astype(F32)
    part_sum = jnp.sum(jnp.where(member, density, 0.0), axis=1, keepdims=True)
    part_count = jnp.sum(jnp.where(member, 1.0, 0.0), axis=1, keepdims=True)
    sums[part] = jnp.where(iota((local_clusters, LANES), 1) == 0, part_sum, part_count)

    def sum_copy(piece, d, home):
        return pltpu.make_async_remote_copy(
            src_ref=sums.at[home], dst_ref=sums.at[home],
            send_sem=sum_send.at[d], recv_sem=sum_recv.at[home],
            device_id=device(me, piece), device_id_type=MESH,
        )

    for d in range(1, parts):
        sum_copy(sibling(d), d, part).start()
    for d in range(1, parts):
        home = sibling(d)
        sum_copy(home, d, home).wait_recv()
    both = sums[0]
    for piece in range(1, parts):
        both = both + sums[piece]
    mean = both[:, 0:1] / jnp.maximum(both[:, 1:2], 1.0)
    row_mean = jnp.sum(jnp.where(member, mean, 0.0), axis=0, keepdims=True)
    final = jnp.where(labels_row > 0.5, density - row_mean, 0.0)
    for l in range(lane_rows):
        result[l] = final[:, l * LANES : (l + 1) * LANES]

    def ret_copy(to, frm):
        return pltpu.make_async_remote_copy(
            src_ref=result.at[to // per_row], dst_ref=returned.at[me],
            send_sem=ret_send.at[to], recv_sem=ret_recv.at[frm],
            device_id=device(to, part), device_id_type=MESH,
        )

    @pl.loop(0, groups - 1, unroll=groups <= 16)
    def _(t):
        ret_copy(peer_out(t), me).start()

    own_ret = pltpu.make_async_copy(result.at[me // per_row], returned.at[me], local_sem.at[2])
    own_ret.start()
    own_ret.wait()

    @pl.loop(0, groups - 1, unroll=groups <= 16)
    def _(t):
        q = peer_in(t)
        id_copy(q, q).wait_send()
        row_copy(q, q).wait_send()

    for d in range(1, parts):
        forward_ids(sibling(d), d, part).wait_send()
        sum_copy(sibling(d), d, part).wait_send()

        @pl.loop(0, groups, unroll=groups <= 16)
        def _(q):
            forward(q, sibling(d), d, part).wait_send()

    @pl.loop(0, groups - 1, unroll=groups <= 16)
    def _(t):
        q = peer_in(t)
        ret_copy(q, q).wait_recv()

    back = jnp.concatenate([returned[g] for g in range(groups)], axis=0)
    picked = dot(back, lane_hit, precision=lax.Precision.HIGHEST)
    out_ref[...] = jnp.sum(owner_hot * picked, axis=0)

    @pl.loop(0, groups - 1, unroll=groups <= 16)
    def _(t):
        q = peer_in(t)
        ret_copy(q, q).wait_send()


def on_device(embeddings, cluster_id, owner_map):
    rows_here, width = embeddings.shape
    clusters_all = owner_map.shape[0]
    groups = lax.axis_size("rows")
    parts = lax.axis_size("split")
    cap = 2 * rows_here // groups
    slots = groups * cap
    lane_rows = slots // LANES
    local_clusters = clusters_all // groups
    dma = pltpu.SemaphoreType.DMA
    regular = pltpu.SemaphoreType.REGULAR
    levels = groups // PLANE
    vmem = pl.BlockSpec(memory_space=pltpu.VMEM)
    out = pl.pallas_call(
        functools.partial(kernel, groups, parts, local_clusters),
        out_shape=jax.ShapeDtypeStruct((rows_here,), F32),
        in_specs=[vmem] * 3,
        out_specs=vmem,
        scratch_shapes=[
            pltpu.VMEM((groups, cap, width), BF16),
            pltpu.VMEM((groups, 1, LANES), F32),
            pltpu.VMEM((parts, groups, cap, width), BF16),
            pltpu.VMEM((parts, groups, 1, LANES), F32),
            pltpu.VMEM((parts, lane_rows, 1, LANES), F32),
            pltpu.VMEM((slots, LANES), F32),
            pltpu.VMEM((parts * slots // KEY_CHUNK, slots, KEY_CHUNK), F32),
            pltpu.VMEM((parts, local_clusters, LANES), F32),
            pltpu.VMEM((lane_rows, 1, LANES), F32),
            pltpu.VMEM((groups, 1, LANES), F32),
            dma((groups,)), dma((groups,)), dma((groups,)), dma((groups,)),
            dma((parts, groups)), dma((parts, groups)), dma((parts,)), dma((parts,)),
            dma((parts,)), dma((parts,)), dma((groups,)), dma((groups,)), dma((3,)),
            regular, regular((levels + 1,)), regular((levels + 1,)),
        ],
        compiler_params=pltpu.CompilerParams(
            collective_id=0, has_side_effects=True, vmem_limit_bytes=60 * 1024 * 1024
        ),
        name="soft_neighbour",
    )(embeddings, cluster_id.reshape(1, rows_here), owner_map.reshape(1, clusters_all))
    return out


def solution(mesh):
    placed = (P(("rows", "split"), None), P(("rows", "split")), P())
    return jax.shard_map(
        on_device, mesh=mesh, in_specs=placed, out_specs=P(("rows", "split")), check_vma=False
    )
```

```python
import functools

import jax
import jax.numpy as jnp
from jax import lax
from jax.experimental import pallas as pl
from jax.experimental.pallas import tpu as pltpu
from jax.sharding import PartitionSpec as P

FLOOR_SCORE = -1e30
LANES = 128
KEY_CHUNK = 256
PLANE = 4
MESH = pl.DeviceIdType.MESH
F32 = jnp.float32
BF16 = jnp.bfloat16


def iota(shape, dim):
    return lax.broadcasted_iota(jnp.int32, shape, dim)


def one_hot(hit, dtype=BF16):
    return jnp.where(hit, 1.0, 0.0).astype(dtype)


def dot(a, b, dims=((1,), (0,)), precision=None):
    return lax.dot_general(a, b, (dims, ((), ())), preferred_element_type=F32, precision=precision)


def column_to_row(column):
    blocks = [
        jnp.transpose(jnp.broadcast_to(column[at : at + LANES], (LANES, LANES)))[0:1]
        for at in range(0, column.shape[0], LANES)
    ]
    return jnp.concatenate(blocks, axis=1)


def kernel(
    groups, parts, local_clusters,
    emb_ref, cid_ref, owner_ref, out_ref,
    outgoing, out_ids, keys, key_ids, id_rows, id_cols, scores, result, returned,
    send_sem, recv_sem, id_send, id_recv, fwd_send, fwd_recv, idf_send, idf_recv,
    ret_send, ret_recv, local_sem, diag_sem, up_sem, down_sem,
):
    rows_here, width = emb_ref.shape
    clusters_all = owner_ref.shape[1]
    cap = outgoing.shape[1]
    per_row = LANES // cap
    slots = groups * cap
    lane_rows = slots // LANES
    r, s = lax.axis_index("rows"), lax.axis_index("split")
    me = (r // parts) * parts + s
    part = r % parts

    def device(group, piece):
        return ((group // parts) * parts + piece, group % parts)

    def step_offset(t):
        half = (t + 1) // 2
        return groups // 2 + half - 2 * half * ((t + 1) % 2)

    def peer_out(t):
        return (me + step_offset(t)) % groups

    def peer_in(t):
        return (me + groups - step_offset(t)) % groups

    def sibling(d):
        return (part + d) % parts

    barrier = pltpu.get_barrier_semaphore()

    levels = groups // PLANE
    z, a, b = me // PLANE, me // 2 % 2, me % 2

    def group_at(level, da, db):
        return level * PLANE + (a + da) % 2 * 2 + (b + db) % 2

    def tell(semaphore, group):
        pl.semaphore_signal(semaphore, inc=1, device_id=device(group, part), device_id_type=MESH)

    def beside(level, action):
        @pl.when((level >= 0) & (level < levels))
        def _():
            action()

    tell(barrier, group_at(z, 1, 0))
    tell(barrier, group_at(z, 0, 1))
    beside(z - 1, lambda: tell(barrier, group_at(z - 1, 0, 0)))
    beside(z + 1, lambda: tell(barrier, group_at(z + 1, 0, 0)))
    for d in range(1, parts):
        pl.semaphore_signal(barrier, inc=1, device_id=device(me, sibling(d)), device_id_type=MESH)

    cid = cid_ref[...]
    cluster_hit = one_hot(iota((clusters_all, rows_here), 0) == cid)
    owner_cl = iota((groups, clusters_all), 0) == owner_ref[...]
    owner_cl_hot = one_hot(owner_cl)
    before_cl = one_hot(iota((clusters_all, clusters_all), 0) < iota((clusters_all, clusters_all), 1))
    local_rank = dot(owner_cl_hot, before_cl)
    label_cl = jnp.where(owner_cl, local_rank + 1.0, 0.0).astype(BF16)
    labels = dot(label_cl, cluster_hit)
    owner_hot = jnp.where(labels > 0.5, 1.0, 0.0)
    before = one_hot(iota((rows_here, rows_here), 0) < iota((rows_here, rows_here), 1))
    prefix = dot(owner_hot.astype(BF16), before)
    rank = jnp.sum(owner_hot * prefix, axis=0, keepdims=True).astype(jnp.int32)
    lane_hit = one_hot(iota((LANES, rows_here), 0) == rank + (me % per_row) * cap, F32)
    id_block = dot(labels.astype(BF16), lane_hit.astype(BF16), ((1,), (1,)))
    for g in range(groups):
        out_ids[g] = id_block[g : g + 1]
    label = jnp.sum(labels, axis=0, keepdims=True).astype(jnp.int32)
    local_hit = one_hot(iota((LANES, rows_here), 0) + 1 == label, F32)
    rank_hot = one_hot(iota((cap, rows_here), 0) == rank, F32)
    emb = emb_ref[...]
    per_step = max(1, 256 // cap)
    for g0 in range(0, groups, per_step):
        placed = jnp.concatenate(
            [(rank_hot * owner_hot[g : g + 1]).astype(BF16) for g in range(g0, min(g0 + per_step, groups))], axis=0
        )
        outgoing[g0 : g0 + per_step] = dot(placed, emb).astype(BF16).reshape(per_step, cap, width)

    def row_copy(to, frm):
        return pltpu.make_async_remote_copy(
            src_ref=outgoing.at[to], dst_ref=keys.at[part, me],
            send_sem=send_sem.at[to], recv_sem=recv_sem.at[frm],
            device_id=device(to, part), device_id_type=MESH,
        )

    def id_copy(to, frm):
        return pltpu.make_async_remote_copy(
            src_ref=out_ids.at[to], dst_ref=key_ids.at[part, me],
            send_sem=id_send.at[to], recv_sem=id_recv.at[frm],
            device_id=device(to, part), device_id_type=MESH,
        )

    def forward(q, piece, d, home):
        return pltpu.make_async_remote_copy(
            src_ref=keys.at[home, q], dst_ref=keys.at[home, q],
            send_sem=fwd_send.at[d, q], recv_sem=fwd_recv.at[home, q],
            device_id=device(me, piece), device_id_type=MESH,
        )

    def forward_ids(piece, d, home):
        return pltpu.make_async_remote_copy(
            src_ref=key_ids.at[home], dst_ref=key_ids.at[home],
            send_sem=idf_send.at[d], recv_sem=idf_recv.at[home],
            device_id=device(me, piece), device_id_type=MESH,
        )

    def send(group):
        id_copy(group, me).start()
        row_copy(group, me).start()

    pl.semaphore_wait(
        barrier, parts + 1 + jnp.where(z > 0, 1, 0) + jnp.where(z < levels - 1, 1, 0)
    )
    beside(z - 1, lambda: send(group_at(z - 1, 0, 0)))
    beside(z + 1, lambda: send(group_at(z + 1, 0, 0)))
    tell(diag_sem, group_at(z, 1, 0))
    send(group_at(z, 1, 0))
    send(group_at(z, 0, 1))
    pl.semaphore_wait(diag_sem, 1)
    beside(z + 1, lambda: tell(up_sem.at[1], group_at(z + 1, 0, 0)))
    beside(z - 1, lambda: tell(down_sem.at[1], group_at(z - 1, 0, 0)))
    send(group_at(z, 1, 1))

    @pl.loop(1, levels, unroll=levels <= 4)
    def _(d):
        def reach(ready, level, onward):
            pl.semaphore_wait(ready.at[d], 1)
            beside(onward, lambda: tell(ready.at[d + 1], group_at(onward, 0, 0)))

            @pl.when(d > 1)
            def _():
                id_copy(group_at(level, 0, 0), me).start()

            for da, db in ((1, 0), (0, 1), (1, 1)):
                id_copy(group_at(level, da, db), me).start()

            @pl.when(d == 1)
            def _():
                row_copy(group_at(level, 1, 0), me).start()

            @pl.when(d > 1)
            def _():
                for da, db in ((1, 1), (0, 0), (1, 0), (0, 1)):
                    row_copy(group_at(level, da, db), me).start()

        beside(z - d, lambda: reach(up_sem, z - d, z + 1))
        beside(z + d, lambda: reach(down_sem, z + d, z - 1))

    def send_rest(level):
        row_copy(group_at(level, 1, 1), me).start()
        row_copy(group_at(level, 0, 1), me).start()

    beside(z - 1, lambda: send_rest(z - 1))
    beside(z + 1, lambda: send_rest(z + 1))

    own_rows = pltpu.make_async_copy(outgoing.at[me], keys.at[part, me], local_sem.at[0])
    own_ids = pltpu.make_async_copy(out_ids.at[me], key_ids.at[part, me], local_sem.at[1])
    own_rows.start()
    own_ids.start()
    own_rows.wait()
    own_ids.wait()
    for d in range(1, parts):
        forward(me, sibling(d), d, part).start()

    def take(q):
        row_copy(q, q).wait_recv()
        for d in range(1, parts):
            forward(q, sibling(d), d, part).start()

    for da, db in ((1, 0), (0, 1), (1, 1)):
        take(group_at(z, da, db))

    @pl.loop(0, groups - 1, unroll=groups <= 16)
    def _(t):
        q = peer_in(t)
        id_copy(q, q).wait_recv()

    for d in range(1, parts):
        forward_ids(sibling(d), d, part).start()
    for d in range(1, parts):
        home = sibling(d)
        forward_ids(home, d, home).wait_recv()

    for piece in range(parts):
        for l in range(lane_rows):
            row = key_ids[piece, l * per_row]
            for j in range(1, per_row):
                row = row + key_ids[piece, l * per_row + j]
            id_rows[piece, l] = row
    query_rows = []
    for l in range(lane_rows):
        row = id_rows[part, l]
        query_rows.append(row)
        id_cols[l * LANES : (l + 1) * LANES] = jnp.transpose(jnp.broadcast_to(row, (LANES, LANES)))

    @pl.loop(1, levels, unroll=levels <= 4)
    def _(d):
        def take_level(level):
            for da, db in ((0, 0), (1, 0), (0, 1), (1, 1)):
                take(group_at(level, da, db))

        beside(z - d, lambda: take_level(z - d))
        beside(z + d, lambda: take_level(z + d))

    for d in range(1, parts):
        home = sibling(d)

        @pl.loop(0, groups, unroll=groups <= 16)
        def _(q):
            forward(q, home, d, home).wait_recv()

    scale = 1.0 / width**0.5
    chunk_groups = KEY_CHUNK // cap
    chunk_lanes = KEY_CHUNK // LANES
    per_piece = groups // chunk_groups
    n_chunks = parts * per_piece

    queries = keys[part].reshape(slots, width)
    id_col = jnp.concatenate([id_cols[...]] * chunk_lanes, axis=1)
    gap = iota((slots, KEY_CHUNK), 0) - iota((slots, KEY_CHUNK), 1)

    def score_chunk(j, high):
        piece, at = j // per_piece, j % per_piece
        block = keys[piece, pl.ds(at * chunk_groups, chunk_groups)].reshape(KEY_CHUNK, width)
        raw = dot(queries, block, ((1,), (1,))) * scale
        id_row = jnp.concatenate([id_rows[piece, at * chunk_lanes + i] for i in range(chunk_lanes)], axis=1)
        own_gap = (piece - part) * slots + at * KEY_CHUNK
        masked = jnp.where((id_col == id_row) & (gap != own_gap), raw, FLOOR_SCORE)
        scores[j] = masked
        folded = masked[:, :LANES]
        for i in range(1, chunk_lanes):
            folded = jnp.maximum(folded, masked[:, i * LANES : (i + 1) * LANES])
        return jnp.maximum(high, folded)

    high = lax.fori_loop(
        0, n_chunks, score_chunk, jnp.full((slots, LANES), FLOOR_SCORE, F32), unroll=n_chunks <= 4
    )
    highest = jnp.max(high, axis=1, keepdims=True)

    def sum_chunk(j, total):
        value = jnp.exp(scores[j] - highest)
        for i in range(chunk_lanes):
            total = total + value[:, i * LANES : (i + 1) * LANES]
        return total

    total = lax.fori_loop(0, n_chunks, sum_chunk, jnp.zeros((slots, LANES), F32), unroll=n_chunks <= 4)
    density = column_to_row(highest + jnp.log(jnp.sum(total, axis=1, keepdims=True)))
    labels_row = jnp.concatenate(query_rows, axis=1)
    member = labels_row == (iota((local_clusters, slots), 0) + 1).astype(F32)
    part_sum = jnp.sum(jnp.where(member, density, 0.0), axis=1, keepdims=True)
    part_count = jnp.sum(jnp.where(member, 1.0, 0.0), axis=1, keepdims=True)
    diagonal = iota((local_clusters, LANES), 0) == iota((local_clusters, LANES), 1)
    sum_row = jnp.sum(jnp.where(diagonal, part_sum, 0.0), axis=0, keepdims=True)
    count_row = jnp.sum(jnp.where(diagonal, part_count, 0.0), axis=0, keepdims=True)
    kept = jnp.where(labels_row > 0.5, density, 0.0)
    for l in range(lane_rows):
        result[l] = jnp.concatenate(
            [kept[:, l * LANES : (l + 1) * LANES], sum_row, count_row, count_row], axis=0
        )

    def ret_copy(to, piece, home, frm):
        return pltpu.make_async_remote_copy(
            src_ref=result.at[to // per_row], dst_ref=returned.at[part, me],
            send_sem=ret_send.at[piece, to], recv_sem=ret_recv.at[home, frm],
            device_id=device(to, piece), device_id_type=MESH,
        )

    @pl.loop(0, groups - 1, unroll=groups <= 16)
    def _(t):
        for d in range(parts):
            ret_copy(peer_out(t), sibling(d), part, me).start()

    for d in range(1, parts):
        ret_copy(me, sibling(d), part, me).start()

    own_ret = pltpu.make_async_copy(result.at[me // per_row], returned.at[part, me], local_sem.at[2])
    own_ret.start()
    own_ret.wait()

    @pl.loop(0, groups - 1, unroll=groups <= 16)
    def _(t):
        q = peer_in(t)
        id_copy(q, q).wait_send()
        row_copy(q, q).wait_send()

    for d in range(1, parts):
        forward_ids(sibling(d), d, part).wait_send()

        @pl.loop(0, groups, unroll=groups <= 16)
        def _(q):
            forward(q, sibling(d), d, part).wait_send()

    @pl.loop(0, groups - 1, unroll=groups <= 16)
    def _(t):
        q = peer_in(t)
        for d in range(parts):
            ret_copy(q, sibling(d), sibling(d), q).wait_recv()

    for d in range(1, parts):
        ret_copy(me, sibling(d), sibling(d), me).wait_recv()

    back = jnp.concatenate([returned[part, g, 0:1] for g in range(groups)], axis=0)
    total_sum = jnp.concatenate([returned[0, g, 1:2] for g in range(groups)], axis=0)
    total_count = jnp.concatenate([returned[0, g, 2:3] for g in range(groups)], axis=0)
    for piece in range(1, parts):
        total_sum += jnp.concatenate([returned[piece, g, 1:2] for g in range(groups)], axis=0)
        total_count += jnp.concatenate([returned[piece, g, 2:3] for g in range(groups)], axis=0)
    mean = total_sum / jnp.maximum(total_count, 1.0)
    picked = dot(
        jnp.concatenate([back, -mean], axis=1),
        jnp.concatenate([lane_hit, local_hit], axis=0),
        precision=lax.Precision.HIGHEST,
    )
    out_ref[...] = jnp.sum(owner_hot * picked, axis=0)

    @pl.loop(0, groups - 1, unroll=groups <= 16)
    def _(t):
        q = peer_in(t)
        for d in range(parts):
            ret_copy(q, sibling(d), sibling(d), q).wait_send()

    for d in range(1, parts):
        ret_copy(me, sibling(d), sibling(d), me).wait_send()


def on_device(embeddings, cluster_id, owner_map):
    rows_here, width = embeddings.shape
    clusters_all = owner_map.shape[0]
    groups = lax.axis_size("rows")
    parts = lax.axis_size("split")
    cap = 2 * rows_here // groups
    slots = groups * cap
    lane_rows = slots // LANES
    local_clusters = clusters_all // groups
    dma = pltpu.SemaphoreType.DMA
    regular = pltpu.SemaphoreType.REGULAR
    levels = groups // PLANE
    vmem = pl.BlockSpec(memory_space=pltpu.VMEM)
    out = pl.pallas_call(
        functools.partial(kernel, groups, parts, local_clusters),
        out_shape=jax.ShapeDtypeStruct((rows_here,), F32),
        in_specs=[vmem] * 3,
        out_specs=vmem,
        scratch_shapes=[
            pltpu.VMEM((groups, cap, width), BF16),
            pltpu.VMEM((groups, 1, LANES), F32),
            pltpu.VMEM((parts, groups, cap, width), BF16),
            pltpu.VMEM((parts, groups, 1, LANES), F32),
            pltpu.VMEM((parts, lane_rows, 1, LANES), F32),
            pltpu.VMEM((slots, LANES), F32),
            pltpu.VMEM((parts * slots // KEY_CHUNK, slots, KEY_CHUNK), F32),
            pltpu.VMEM((lane_rows, 4, LANES), F32),
            pltpu.VMEM((parts, groups, 4, LANES), F32),
            dma((groups,)), dma((groups,)), dma((groups,)), dma((groups,)),
            dma((parts, groups)), dma((parts, groups)), dma((parts,)), dma((parts,)),
            dma((parts, groups)), dma((parts, groups)), dma((3,)),
            regular, regular((levels + 1,)), regular((levels + 1,)),
        ],
        compiler_params=pltpu.CompilerParams(
            collective_id=0, has_side_effects=True, vmem_limit_bytes=60 * 1024 * 1024
        ),
        name="soft_neighbour",
    )(embeddings, cluster_id.reshape(1, rows_here), owner_map.reshape(1, clusters_all))
    return out


def solution(mesh):
    placed = (P(("rows", "split"), None), P(("rows", "split")), P())
    return jax.shard_map(
        on_device, mesh=mesh, in_specs=placed, out_specs=P(("rows", "split")), check_vma=False
    )
```

```python
import functools

import jax
import jax.numpy as jnp
from jax import lax
from jax.experimental import pallas as pl
from jax.experimental.pallas import tpu as pltpu
from jax.sharding import PartitionSpec as P

FLOOR_SCORE = -1e30
LANES = 128
KEY_CHUNK = 256
PLANE = 4
MESH = pl.DeviceIdType.MESH
F32 = jnp.float32
BF16 = jnp.bfloat16


def iota(shape, dim):
    return lax.broadcasted_iota(jnp.int32, shape, dim)


def one_hot(hit, dtype=BF16):
    return jnp.where(hit, 1.0, 0.0).astype(dtype)


def dot(a, b, dims=((1,), (0,)), precision=None):
    return lax.dot_general(a, b, (dims, ((), ())), preferred_element_type=F32, precision=precision)


def column_to_row(column):
    blocks = [
        jnp.transpose(jnp.broadcast_to(column[at : at + LANES], (LANES, LANES)))[0:1]
        for at in range(0, column.shape[0], LANES)
    ]
    return jnp.concatenate(blocks, axis=1)


def kernel(
    groups, parts, local_clusters,
    emb_in, cid_in, owner_in, out_ref,
    emb_ref, cid_ref, owner_ref,
    outgoing, out_ids, keys, key_ids, id_rows, id_cols, scores, result, returned,
    send_sem, recv_sem, id_send, id_recv, fwd_send, fwd_recv, idf_send, idf_recv,
    ret_send, ret_recv, local_sem, diag_sem, up_sem, down_sem, load_sem,
):
    rows_here, width = emb_ref.shape
    clusters_all = owner_ref.shape[1]
    cap = outgoing.shape[1]
    per_row = LANES // cap
    slots = groups * cap
    lane_rows = slots // LANES
    r, s = lax.axis_index("rows"), lax.axis_index("split")
    me = (r // parts) * parts + s
    part = r % parts

    def device(group, piece):
        return ((group // parts) * parts + piece, group % parts)

    def step_offset(t):
        half = (t + 1) // 2
        return groups // 2 + half - 2 * half * ((t + 1) % 2)

    def peer_out(t):
        return (me + step_offset(t)) % groups

    def peer_in(t):
        return (me + groups - step_offset(t)) % groups

    def sibling(d):
        return (part + d) % parts

    barrier = pltpu.get_barrier_semaphore()

    levels = groups // PLANE
    z, a, b = me // PLANE, me // 2 % 2, me % 2

    def group_at(level, da, db):
        return level * PLANE + (a + da) % 2 * 2 + (b + db) % 2

    def tell(semaphore, group):
        pl.semaphore_signal(semaphore, inc=1, device_id=device(group, part), device_id_type=MESH)

    def beside(level, action):
        @pl.when((level >= 0) & (level < levels))
        def _():
            action()

    tell(barrier, group_at(z, 1, 0))
    tell(barrier, group_at(z, 0, 1))
    beside(z - 1, lambda: tell(barrier, group_at(z - 1, 0, 0)))
    beside(z + 1, lambda: tell(barrier, group_at(z + 1, 0, 0)))
    for d in range(1, parts):
        pl.semaphore_signal(barrier, inc=1, device_id=device(me, sibling(d)), device_id_type=MESH)

    loads = [
        pltpu.make_async_copy(given, held, load_sem.at[i])
        for i, (given, held) in enumerate(((cid_in, cid_ref), (owner_in, owner_ref), (emb_in, emb_ref)))
    ]
    for load in loads:
        load.start()
    loads[0].wait()
    loads[1].wait()

    cid = cid_ref[...]
    cluster_hit = one_hot(iota((clusters_all, rows_here), 0) == cid)
    owner_cl = iota((groups, clusters_all), 0) == owner_ref[...]
    owner_cl_hot = one_hot(owner_cl)
    before_cl = one_hot(iota((clusters_all, clusters_all), 0) < iota((clusters_all, clusters_all), 1))
    local_rank = dot(owner_cl_hot, before_cl)
    label_cl = jnp.where(owner_cl, local_rank + 1.0, 0.0).astype(BF16)
    labels = dot(label_cl, cluster_hit)
    owner_hot = jnp.where(labels > 0.5, 1.0, 0.0)
    before = one_hot(iota((rows_here, rows_here), 0) < iota((rows_here, rows_here), 1))
    prefix = dot(owner_hot.astype(BF16), before)
    rank = jnp.sum(owner_hot * prefix, axis=0, keepdims=True).astype(jnp.int32)
    lane_hit = one_hot(iota((LANES, rows_here), 0) == rank + (me % per_row) * cap, F32)
    id_block = dot(labels.astype(BF16), lane_hit.astype(BF16), ((1,), (1,)))
    for g in range(groups):
        out_ids[g] = id_block[g : g + 1]
    label = jnp.sum(labels, axis=0, keepdims=True).astype(jnp.int32)
    local_hit = one_hot(iota((LANES, rows_here), 0) + 1 == label, F32)
    rank_hot = one_hot(iota((cap, rows_here), 0) == rank, F32)
    loads[2].wait()
    emb = emb_ref[...]
    per_step = max(1, 256 // cap)
    for g0 in range(0, groups, per_step):
        placed = jnp.concatenate(
            [(rank_hot * owner_hot[g : g + 1]).astype(BF16) for g in range(g0, min(g0 + per_step, groups))], axis=0
        )
        outgoing[g0 : g0 + per_step] = dot(placed, emb).astype(BF16).reshape(per_step, cap, width)

    def row_copy(to, frm):
        return pltpu.make_async_remote_copy(
            src_ref=outgoing.at[to], dst_ref=keys.at[part, me],
            send_sem=send_sem.at[to], recv_sem=recv_sem.at[frm],
            device_id=device(to, part), device_id_type=MESH,
        )

    def id_copy(to, frm):
        return pltpu.make_async_remote_copy(
            src_ref=out_ids.at[to], dst_ref=key_ids.at[part, me],
            send_sem=id_send.at[to], recv_sem=id_recv.at[frm],
            device_id=device(to, part), device_id_type=MESH,
        )

    def forward(q, piece, d, home):
        return pltpu.make_async_remote_copy(
            src_ref=keys.at[home, q], dst_ref=keys.at[home, q],
            send_sem=fwd_send.at[d, q], recv_sem=fwd_recv.at[home, q],
            device_id=device(me, piece), device_id_type=MESH,
        )

    def forward_ids(piece, d, home):
        return pltpu.make_async_remote_copy(
            src_ref=key_ids.at[home], dst_ref=key_ids.at[home],
            send_sem=idf_send.at[d], recv_sem=idf_recv.at[home],
            device_id=device(me, piece), device_id_type=MESH,
        )

    def send(group):
        id_copy(group, me).start()
        row_copy(group, me).start()

    pl.semaphore_wait(
        barrier, parts + 1 + jnp.where(z > 0, 1, 0) + jnp.where(z < levels - 1, 1, 0)
    )
    beside(z - 1, lambda: send(group_at(z - 1, 0, 0)))
    beside(z + 1, lambda: send(group_at(z + 1, 0, 0)))
    tell(diag_sem, group_at(z, 1, 0))
    send(group_at(z, 1, 0))
    send(group_at(z, 0, 1))
    pl.semaphore_wait(diag_sem, 1)
    beside(z + 1, lambda: tell(up_sem.at[1], group_at(z + 1, 0, 0)))
    beside(z - 1, lambda: tell(down_sem.at[1], group_at(z - 1, 0, 0)))
    send(group_at(z, 1, 1))

    @pl.loop(1, levels, unroll=levels <= 4)
    def _(d):
        def reach(ready, level, onward):
            pl.semaphore_wait(ready.at[d], 1)
            beside(onward, lambda: tell(ready.at[d + 1], group_at(onward, 0, 0)))

            @pl.when(d > 1)
            def _():
                id_copy(group_at(level, 0, 0), me).start()

            for da, db in ((1, 0), (0, 1), (1, 1)):
                id_copy(group_at(level, da, db), me).start()

            @pl.when(d == 1)
            def _():
                row_copy(group_at(level, 1, 0), me).start()

            @pl.when(d > 1)
            def _():
                for da, db in ((1, 1), (0, 0), (1, 0), (0, 1)):
                    row_copy(group_at(level, da, db), me).start()

        beside(z - d, lambda: reach(up_sem, z - d, z + 1))
        beside(z + d, lambda: reach(down_sem, z + d, z - 1))

    def send_rest(level):
        row_copy(group_at(level, 1, 1), me).start()
        row_copy(group_at(level, 0, 1), me).start()

    beside(z - 1, lambda: send_rest(z - 1))
    beside(z + 1, lambda: send_rest(z + 1))

    own_rows = pltpu.make_async_copy(outgoing.at[me], keys.at[part, me], local_sem.at[0])
    own_ids = pltpu.make_async_copy(out_ids.at[me], key_ids.at[part, me], local_sem.at[1])
    own_rows.start()
    own_ids.start()
    own_rows.wait()
    own_ids.wait()
    for d in range(1, parts):
        forward(me, sibling(d), d, part).start()

    def take(q):
        row_copy(q, q).wait_recv()
        for d in range(1, parts):
            forward(q, sibling(d), d, part).start()

    for da, db in ((1, 0), (0, 1), (1, 1)):
        take(group_at(z, da, db))

    @pl.loop(0, groups - 1, unroll=groups <= 16)
    def _(t):
        q = peer_in(t)
        id_copy(q, q).wait_recv()

    for d in range(1, parts):
        forward_ids(sibling(d), d, part).start()
    for d in range(1, parts):
        home = sibling(d)
        forward_ids(home, d, home).wait_recv()

    for piece in range(parts):
        for l in range(lane_rows):
            row = key_ids[piece, l * per_row]
            for j in range(1, per_row):
                row = row + key_ids[piece, l * per_row + j]
            id_rows[piece, l] = row
    query_rows = []
    for l in range(lane_rows):
        row = id_rows[part, l]
        query_rows.append(row)
        id_cols[l * LANES : (l + 1) * LANES] = jnp.transpose(jnp.broadcast_to(row, (LANES, LANES)))

    @pl.loop(1, levels, unroll=levels <= 4)
    def _(d):
        def take_level(level):
            for da, db in ((0, 0), (1, 0), (0, 1), (1, 1)):
                take(group_at(level, da, db))

        beside(z - d, lambda: take_level(z - d))
        beside(z + d, lambda: take_level(z + d))

    for d in range(1, parts):
        home = sibling(d)

        @pl.loop(0, groups, unroll=groups <= 16)
        def _(q):
            forward(q, home, d, home).wait_recv()

    scale = 1.0 / width**0.5
    chunk_groups = KEY_CHUNK // cap
    chunk_lanes = KEY_CHUNK // LANES
    per_piece = groups // chunk_groups
    n_chunks = parts * per_piece

    queries = keys[part].reshape(slots, width)
    id_col = jnp.concatenate([id_cols[...]] * chunk_lanes, axis=1)
    gap = iota((slots, KEY_CHUNK), 0) - iota((slots, KEY_CHUNK), 1)

    def score_chunk(j, high):
        piece, at = j // per_piece, j % per_piece
        block = keys[piece, pl.ds(at * chunk_groups, chunk_groups)].reshape(KEY_CHUNK, width)
        raw = dot(queries, block, ((1,), (1,))) * scale
        id_row = jnp.concatenate([id_rows[piece, at * chunk_lanes + i] for i in range(chunk_lanes)], axis=1)
        own_gap = (piece - part) * slots + at * KEY_CHUNK
        masked = jnp.where((id_col == id_row) & (gap != own_gap), raw, FLOOR_SCORE)
        scores[j] = masked
        folded = masked[:, :LANES]
        for i in range(1, chunk_lanes):
            folded = jnp.maximum(folded, masked[:, i * LANES : (i + 1) * LANES])
        return jnp.maximum(high, folded)

    high = lax.fori_loop(
        0, n_chunks, score_chunk, jnp.full((slots, LANES), FLOOR_SCORE, F32), unroll=n_chunks <= 4
    )
    highest = jnp.max(high, axis=1, keepdims=True)

    def sum_chunk(j, total):
        value = jnp.exp(scores[j] - highest)
        for i in range(chunk_lanes):
            total = total + value[:, i * LANES : (i + 1) * LANES]
        return total

    total = lax.fori_loop(0, n_chunks, sum_chunk, jnp.zeros((slots, LANES), F32), unroll=n_chunks <= 4)
    density = column_to_row(highest + jnp.log(jnp.sum(total, axis=1, keepdims=True)))
    labels_row = jnp.concatenate(query_rows, axis=1)
    member = labels_row == (iota((local_clusters, slots), 0) + 1).astype(F32)
    part_sum = jnp.sum(jnp.where(member, density, 0.0), axis=1, keepdims=True)
    part_count = jnp.sum(jnp.where(member, 1.0, 0.0), axis=1, keepdims=True)
    diagonal = iota((local_clusters, LANES), 0) == iota((local_clusters, LANES), 1)
    sum_row = jnp.sum(jnp.where(diagonal, part_sum, 0.0), axis=0, keepdims=True)
    count_row = jnp.sum(jnp.where(diagonal, part_count, 0.0), axis=0, keepdims=True)
    kept = jnp.where(labels_row > 0.5, density, 0.0)
    for l in range(lane_rows):
        result[l] = jnp.concatenate(
            [kept[:, l * LANES : (l + 1) * LANES], sum_row, count_row, count_row], axis=0
        )

    def ret_copy(to, piece, home, frm):
        return pltpu.make_async_remote_copy(
            src_ref=result.at[to // per_row], dst_ref=returned.at[part, me],
            send_sem=ret_send.at[piece, to], recv_sem=ret_recv.at[home, frm],
            device_id=device(to, piece), device_id_type=MESH,
        )

    @pl.loop(0, groups - 1, unroll=groups <= 16)
    def _(t):
        for d in range(parts):
            ret_copy(peer_out(t), sibling(d), part, me).start()

    for d in range(1, parts):
        ret_copy(me, sibling(d), part, me).start()

    own_ret = pltpu.make_async_copy(result.at[me // per_row], returned.at[part, me], local_sem.at[2])
    own_ret.start()
    own_ret.wait()

    @pl.loop(0, groups - 1, unroll=groups <= 16)
    def _(t):
        q = peer_in(t)
        id_copy(q, q).wait_send()
        row_copy(q, q).wait_send()

    for d in range(1, parts):
        forward_ids(sibling(d), d, part).wait_send()

        @pl.loop(0, groups, unroll=groups <= 16)
        def _(q):
            forward(q, sibling(d), d, part).wait_send()

    @pl.loop(0, groups - 1, unroll=groups <= 16)
    def _(t):
        q = peer_in(t)
        for d in range(parts):
            ret_copy(q, sibling(d), sibling(d), q).wait_recv()

    for d in range(1, parts):
        ret_copy(me, sibling(d), sibling(d), me).wait_recv()

    back = jnp.concatenate([returned[part, g, 0:1] for g in range(groups)], axis=0)
    total_sum = jnp.concatenate([returned[0, g, 1:2] for g in range(groups)], axis=0)
    total_count = jnp.concatenate([returned[0, g, 2:3] for g in range(groups)], axis=0)
    for piece in range(1, parts):
        total_sum += jnp.concatenate([returned[piece, g, 1:2] for g in range(groups)], axis=0)
        total_count += jnp.concatenate([returned[piece, g, 2:3] for g in range(groups)], axis=0)
    mean = total_sum / jnp.maximum(total_count, 1.0)
    picked = dot(
        jnp.concatenate([back, -mean], axis=1),
        jnp.concatenate([lane_hit, local_hit], axis=0),
        precision=lax.Precision.HIGHEST,
    )
    out_ref[...] = jnp.sum(owner_hot * picked, axis=0)

    @pl.loop(0, groups - 1, unroll=groups <= 16)
    def _(t):
        q = peer_in(t)
        for d in range(parts):
            ret_copy(q, sibling(d), sibling(d), q).wait_send()

    for d in range(1, parts):
        ret_copy(me, sibling(d), sibling(d), me).wait_send()


def on_device(embeddings, cluster_id, owner_map):
    rows_here, width = embeddings.shape
    clusters_all = owner_map.shape[0]
    groups = lax.axis_size("rows")
    parts = lax.axis_size("split")
    cap = 2 * rows_here // groups
    slots = groups * cap
    lane_rows = slots // LANES
    local_clusters = clusters_all // groups
    dma = pltpu.SemaphoreType.DMA
    regular = pltpu.SemaphoreType.REGULAR
    levels = groups // PLANE
    vmem = pl.BlockSpec(memory_space=pltpu.VMEM)
    out = pl.pallas_call(
        functools.partial(kernel, groups, parts, local_clusters),
        out_shape=jax.ShapeDtypeStruct((rows_here,), F32),
        in_specs=[pl.BlockSpec(memory_space=pl.ANY)] * 3,
        out_specs=vmem,
        scratch_shapes=[
            pltpu.VMEM((rows_here, width), BF16),
            pltpu.VMEM((1, rows_here), jnp.int32),
            pltpu.VMEM((1, clusters_all), jnp.int32),
            pltpu.VMEM((groups, cap, width), BF16),
            pltpu.VMEM((groups, 1, LANES), F32),
            pltpu.VMEM((parts, groups, cap, width), BF16),
            pltpu.VMEM((parts, groups, 1, LANES), F32),
            pltpu.VMEM((parts, lane_rows, 1, LANES), F32),
            pltpu.VMEM((slots, LANES), F32),
            pltpu.VMEM((parts * slots // KEY_CHUNK, slots, KEY_CHUNK), F32),
            pltpu.VMEM((lane_rows, 4, LANES), F32),
            pltpu.VMEM((parts, groups, 4, LANES), F32),
            dma((groups,)), dma((groups,)), dma((groups,)), dma((groups,)),
            dma((parts, groups)), dma((parts, groups)), dma((parts,)), dma((parts,)),
            dma((parts, groups)), dma((parts, groups)), dma((3,)),
            regular, regular((levels + 1,)), regular((levels + 1,)), dma((3,)),
        ],
        compiler_params=pltpu.CompilerParams(
            collective_id=0, has_side_effects=True, vmem_limit_bytes=60 * 1024 * 1024
        ),
        name="soft_neighbour",
    )(embeddings, cluster_id.reshape(1, rows_here), owner_map.reshape(1, clusters_all))
    return out


def solution(mesh):
    placed = (P(("rows", "split"), None), P(("rows", "split")), P())
    return jax.shard_map(
        on_device, mesh=mesh, in_specs=placed, out_specs=P(("rows", "split")), check_vma=False
    )
```
